32 devices in a mesh: layer: 2 (over core), energy: 4 (over y, x), momentum: 4 (over z).
Axes of the slice: x: 2, y: 2, z: 4, core: 2. Of those that a mesh axis runs over, the one named last changes fastest.
Arguments:
- diag_blocks: float32 [4, 4, 4, 2, 384, 384], P('momentum', 'layer', 'energy'), may hold values from -1 to 5
- couplings: float32 [4, 4, 2, 384, 384], P('momentum', 'layer'), may hold values from -0.15625 to 0.15625
- phonon_matrix: float32 [4, 4], replicated, may hold values from -3 to 3
- mode_strength: float32 [3], replicated, may hold values from 0.5 to 2
- transfer_mode: int32 [4], replicated, may hold values from 0 to 2, as said below
- energy_offset: int32 [3], replicated, may hold values from 0 to 1, as said below
Outputs:
- self_energy: float32 [4, 2, 4, 2, 384, 384], P('momentum', 'layer', 'energy')
The draws below stay inside these ranges and needn't reach their ends.
Inputs may be any that keep to these rules, and one draw needn't show every extreme that they name: `transfer_mode`: every one of the 3 modes is the mode of some transfer. `energy_offset`: some mode has offset 0 and some mode has offset 1.
All inputs are finite; a program needn't handle non-finite values.
Results may differ from the reference program's by a relative error of at most 0.00011.
Values sent between devices are 32-bit elements; how exact they have to be, the bound alone decides.
A program may use at most 64 MiB of HBM per device.

```python
import math
from functools import partial
import jax
import jax.numpy as jnp
from jax import lax

B = 384
MODES = 3
LAYERS = 4
NE = 4
NK = 4
OFFMAX = 1


def draw_diag_blocks(key, part):
    base = jax.random.fold_in(key, 101)
    first_key, second_key, third_key = jax.random.split(base, 3)
    off_scale = 0.4 * math.sqrt(2.0) / math.sqrt(B)
    real_diag = jnp.exp(jax.random.uniform(first_key, (NK, LAYERS, NE, B), jnp.float32, math.log(2.0), math.log(4.0)))
    imag_diag = jax.random.uniform(second_key, (NK, LAYERS, NE, B), jnp.float32, 0.6, 1.2)
    noise = jnp.clip(jax.random.normal(third_key, (NK, LAYERS, NE, 2, B, B), jnp.float32), -4.0, 4.0) * off_scale
    noise_real = noise[..., 0, :, :]
    noise_imag = noise[..., 1, :, :]
    herm_real = 0.5 * (noise_real + jnp.swapaxes(noise_real, -1, -2))
    herm_imag = 0.5 * (noise_imag - jnp.swapaxes(noise_imag, -1, -2))
    identity = jnp.eye(B, dtype=jnp.float32)
    block_real = herm_real + identity * real_diag[..., None]
    block_imag = herm_imag + identity * imag_diag[..., None]
    return jnp.stack([block_real, block_imag], axis=-3).astype(jnp.float32)


def draw_transfer_mode(key, part):
    base = jax.random.fold_in(key, 202)
    return jax.random.permutation(base, jnp.arange(NK, dtype=jnp.int32) % MODES).astype(jnp.int32)


def draw_energy_offset(key, part):
    base = jax.random.fold_in(key, 303)
    first_key, second_key = jax.random.split(base, 2)
    values = jax.random.randint(first_key, (MODES,), 0, OFFMAX + 1, dtype=jnp.int32)
    order = jax.random.permutation(second_key, MODES)
    values = values.at[order[0]].set(0)
    values = values.at[order[1]].set(OFFMAX)
    return values.astype(jnp.int32)


def level_of(stream_key, dims, pieces, low, largest):
    gain, own = 1.0, jax.random.fold_in(stream_key, 6)
    for axis_at, parts in pieces:
        draws = jnp.exp(jax.random.uniform(jax.random.fold_in(own, axis_at), (parts,), jnp.float32, low / len(pieces), largest / len(pieces)))
        gain = gain * jnp.repeat(draws, dims[axis_at] // parts).reshape([-1 if axis == axis_at else 1 for axis in range(len(dims))])
    return gain


def gaussian(stream_key, dims, deviation, reach, pieces=(), kind=jnp.bfloat16):
    values = deviation * jax.random.normal(stream_key, dims, jnp.float32)
    if pieces:
        values = values * level_of(stream_key, dims, pieces, -0.22, 0.18)
    return jnp.clip(values, -reach, reach).astype(kind)


def setup_inputs(seed: int = 0) -> dict:
    streams_of = jax.random.split(jax.random.key(seed), 7)
    diag_blocks = draw_diag_blocks(jax.random.fold_in(streams_of[6], 71), 0)
    couplings = gaussian(streams_of[1], (NK, LAYERS, 2, B, B), (4 * B) ** -0.5, 0.15625, ((0, 4), (1, 2)), jnp.float32)
    phonon_matrix = gaussian(streams_of[2], (NE, NE), NE ** -0.5, 3.0, (), jnp.float32)
    mode_strength = jnp.clip(jnp.exp(jax.random.uniform(streams_of[3], (MODES,), jnp.float32, math.log(0.5), math.log(2.0))), 0.5, 2.0)
    transfer_mode = draw_transfer_mode(jax.random.fold_in(streams_of[6], 71), 0)
    energy_offset = draw_energy_offset(jax.random.fold_in(streams_of[6], 71), 0)
    return dict(diag_blocks=diag_blocks, couplings=couplings, phonon_matrix=phonon_matrix, mode_strength=mode_strength, transfer_mode=transfer_mode, energy_offset=energy_offset)


def complex_product(left, right):
    product = partial(jnp.matmul, precision=lax.Precision.HIGHEST)
    real_part = product(left[..., 0, :, :], right[..., 0, :, :]) - product(left[..., 1, :, :], right[..., 1, :, :])
    imag_part = product(left[..., 0, :, :], right[..., 1, :, :]) + product(left[..., 1, :, :], right[..., 0, :, :])
    return jnp.stack([real_part, imag_part], axis=-3)


def adjoint(matrix):
    return jnp.stack([jnp.swapaxes(matrix[..., 0, :, :], -1, -2), -jnp.swapaxes(matrix[..., 1, :, :], -1, -2)], axis=-3)


def refined_inverse(matrix):
    real_diag = jnp.diagonal(matrix[..., 0, :, :], axis1=-2, axis2=-1)
    imag_diag = jnp.diagonal(matrix[..., 1, :, :], axis1=-2, axis2=-1)
    modulus = real_diag * real_diag + imag_diag * imag_diag
    inv_real = real_diag / modulus
    inv_imag = -imag_diag / modulus
    block_order = matrix.shape[-1]
    identity = jnp.eye(block_order, dtype=jnp.float32)
    scaled_real = matrix[..., 0, :, :] * inv_real[..., None, :] - matrix[..., 1, :, :] * inv_imag[..., None, :]
    scaled_imag = matrix[..., 0, :, :] * inv_imag[..., None, :] + matrix[..., 1, :, :] * inv_real[..., None, :]
    resid_real = 2.0 * identity - scaled_real
    resid_imag = -scaled_imag
    first_real = inv_real[..., :, None] * resid_real - inv_imag[..., :, None] * resid_imag
    first_imag = inv_real[..., :, None] * resid_imag + inv_imag[..., :, None] * resid_real
    first = jnp.stack([first_real, first_imag], axis=-3)
    two_identity = jnp.stack([2.0 * identity, jnp.zeros_like(identity)], axis=0)
    residual = two_identity - complex_product(matrix, first)
    return complex_product(first, residual)


def shift_down(values):
    return jnp.concatenate([jnp.zeros_like(values[:1]), values[:-1]], axis=0)


def shift_up(values):
    return jnp.concatenate([values[1:], jnp.zeros_like(values[:1])], axis=0)


def reduce_momentum(operands):
    diag_one, coupling_one = operands
    even_diag = diag_one[0::2]
    odd_diag = diag_one[1::2]
    even_coupling = coupling_one[0::2][:, None]
    odd_coupling = coupling_one[1::2][:, None]
    odd_inverse = refined_inverse(odd_diag)
    even_adjoint = adjoint(even_coupling)
    odd_adjoint = adjoint(odd_coupling)
    left_even = complex_product(even_coupling, odd_inverse)
    left_odd = complex_product(odd_adjoint, odd_inverse)
    own_term = complex_product(left_even, even_adjoint)
    edge_term = complex_product(left_odd, odd_coupling)
    upper = -complex_product(left_even, odd_coupling)
    lower = -complex_product(left_odd, even_adjoint)
    reduced = even_diag - own_term - shift_down(edge_term)
    reduced_inverse = refined_inverse(reduced)
    lower_term = complex_product(complex_product(lower, reduced_inverse), upper)
    upper_term = complex_product(complex_product(upper, shift_up(reduced_inverse)), lower)
    twice = reduced - upper_term - shift_down(lower_term)
    return refined_inverse(twice)


def reference(diag_blocks, couplings, phonon_matrix, mode_strength, transfer_mode, energy_offset):
    greens = lax.map(reduce_momentum, (diag_blocks, couplings))
    folded = jnp.einsum('ef,kjfcrb->kjecrb', phonon_matrix, greens, precision=lax.Precision.HIGHEST)
    energies = jnp.arange(NE, dtype=jnp.int32)
    target = energies[:, None]
    source = energies[None, :]
    total = jnp.zeros_like(folded)
    for transfer in range(NK):
        mode = transfer_mode[transfer]
        offset = energy_offset[mode]
        strength = mode_strength[mode]
        kernel = strength * ((source == target - offset).astype(jnp.float32) + (source == target + offset).astype(jnp.float32))
        total = total + jnp.einsum('ef,kjfcrb->kjecrb', kernel, jnp.roll(folded, transfer, axis=0), precision=lax.Precision.HIGHEST)
    return total
```

```python
from functools import partial

import jax
import jax.numpy as jnp
from jax import lax
from jax.experimental import pallas as pl
from jax.experimental.pallas import tpu as pltpu
from jax.sharding import PartitionSpec as P

MESH = pl.DeviceIdType.MESH
F32 = jnp.float32
BF16 = jnp.bfloat16
LANES = 128


def split(value):
    high = value.astype(BF16)
    low = (value - high.astype(F32)).astype(BF16)
    return high, low


def put_left(left, rows, n, value):
    columns = pl.ds(n * 2 * LANES, 2 * LANES)
    for ref, part in zip(left, split(value)):
        ref[rows, columns] = part


def put_right(right, c, n, value):
    for ref, part in zip(right, split(value)):
        base = c * 2 * LANES
        ref[n, base:base + LANES, :] = part
        ref[n, base + LANES:base + 2 * LANES, :LANES] = -part[:, LANES:]
        ref[n, base + LANES:base + 2 * LANES, LANES:] = part[:, :LANES]


def put_right_all(right, n, value):
    for c in range(value.shape[0] // LANES):
        put_right(right, c, n, value[c * LANES:(c + 1) * LANES])


def dot(a, b):
    return jnp.dot(a, b, preferred_element_type=F32)


def product(left, right, n):
    left_high, left_low = left[0][...], left[1][...]
    right_high, right_low = right[0][n], right[1][n]
    return dot(left_high, right_high) + dot(left_high, right_low) + dot(left_low, right_high)


def kernel(
    chunks, nodes, energies, momenta,
    diag, coup, phonon, strength, transfer, offset, out,
    diag_odd, diag_even, c_even, c_odd, c_odd_left,
    x_own, x_left, lo_send, lo_recv, up_own, up_left, low_own, low_left,
    lt_send, lt_recv, ut_send, ut_recv, reduced, gbuf, rbuf, tbuf, obuf, kern,
    la_h, la_l, lb_h, lb_l, lc_h, lc_l,
    ra_h, ra_l, rb_h, rb_l, rc_h, rc_l,
    in_sem, l_send, l_recv, f_send, f_recv, b_send, b_recv,
):
    la, lb, lc = (la_h, la_l), (lb_h, lb_l), (lc_h, lc_l)
    ra, rb, rc = (ra_h, ra_l), (rb_h, rb_l), (rc_h, rc_l)
    order = chunks * LANES
    me = lax.axis_index("layer")
    here_k = lax.axis_index("momentum")
    here_e = lax.axis_index("energy")
    peers = energies * momenta
    here = here_k * energies + here_e
    rows = order // peers
    has_right = me < nodes - 1
    has_left = me > 0

    loads = []
    for s, (src, dst) in enumerate(
        ((diag.at[1], diag_odd), (coup.at[0], c_even), (coup.at[1], c_odd), (diag.at[0], diag_even))
    ):
        load = pltpu.make_async_copy(src, dst, in_sem.at[s])
        load.start()
        loads.append(load)

    barrier = pltpu.get_barrier_semaphore()

    @pl.when(has_right)
    def _():
        pl.semaphore_signal(barrier, inc=1, device_id={"layer": me + 1}, device_id_type=MESH)

    @pl.when(has_left)
    def _():
        pl.semaphore_signal(barrier, inc=1, device_id={"layer": me - 1}, device_id_type=MESH)

    def greet(d, carry):
        peer = lax.rem(here + d, peers)
        pl.semaphore_signal(
            barrier, inc=1,
            device_id={"momentum": peer // energies, "energy": lax.rem(peer, energies)},
            device_id_type=MESH,
        )
        return carry

    lax.fori_loop(1, peers, greet, 0)

    def to_layer(slot, src, dst, step):
        return pltpu.make_async_remote_copy(
            src_ref=src, dst_ref=dst, send_sem=l_send.at[slot], recv_sem=l_recv.at[slot],
            device_id={"layer": me + step}, device_id_type=MESH,
        )

    send_c = to_layer(0, c_odd, c_odd_left, 1)
    send_x = to_layer(1, x_own, x_left, 1)
    send_lo = to_layer(2, lo_send, lo_recv, -1)
    send_up = to_layer(3, up_own, up_left, 1)
    send_low = to_layer(4, low_own, low_left, 1)
    send_lt = to_layer(5, lt_send, lt_recv, 1)
    send_ut = to_layer(6, ut_send, ut_recv, -1)

    eye = (
        lax.broadcasted_iota(jnp.int32, (LANES, LANES), 0)
        == lax.broadcasted_iota(jnp.int32, (LANES, LANES), 1)
    )
    two = jnp.where(eye, F32(2.0), F32(0.0))

    def prepare_inverse(read):
        row_inv, col_inv = [], []
        for c in range(chunks):
            block = read(c, c)
            real = jnp.where(eye, block[:, :LANES], 0.0)
            imag = jnp.where(eye, block[:, LANES:], 0.0)
            for axis, found in ((0, row_inv), (1, col_inv)):
                r = jnp.sum(real, axis=axis, keepdims=True)
                i = jnp.sum(imag, axis=axis, keepdims=True)
                modulus = r * r + i * i
                found.append((r / modulus, -i / modulus))
        for n in range(chunks):
            for c in range(chunks):
                block = read(c, n)
                put_left(la, slice(c * LANES, (c + 1) * LANES), n, block)
                a_r, a_i = block[:, :LANES], block[:, LANES:]
                x_r, x_i = row_inv[n]
                y_r, y_i = col_inv[c]
                res_r = a_i * x_i - a_r * x_r
                if c == n:
                    res_r = res_r + two
                res_i = -(a_r * x_i + a_i * x_r)
                first = jnp.concatenate(
                    [y_r * res_r - y_i * res_i, y_r * res_i + y_i * res_r], axis=1
                )
                put_left(lb, slice(c * LANES, (c + 1) * LANES), n, first)
                put_right(ra, c, n, first)

    def residual(n):
        acc = product(la, ra, n)
        for c in range(chunks):
            same = jnp.where(n == c, F32(1.0), F32(0.0))
            block = acc[c * LANES:(c + 1) * LANES]
            block = jnp.concatenate([two * same - block[:, :LANES], -block[:, LANES:]], axis=1)
            put_right(rb, c, n, block)

    def each(fn):
        lax.fori_loop(0, chunks, lambda n, carry: (fn(n), carry)[1], 0)

    def pair_block(ref, c, n):
        rs, cs = slice(c * LANES, (c + 1) * LANES), slice(n * LANES, (n + 1) * LANES)
        return jnp.concatenate([ref[0, rs, cs], ref[1, rs, cs]], axis=1)

    def adjoint_block(ref, c, n):
        rs, cs = slice(n * LANES, (n + 1) * LANES), slice(c * LANES, (c + 1) * LANES)
        return jnp.concatenate([ref[0, rs, cs].T, -ref[1, rs, cs].T], axis=1)

    every = slice(0, order)

    loads[0].wait()
    prepare_inverse(lambda c, n: pair_block(diag_odd, c, n))
    each(residual)

    neighbours = jnp.where(has_left, 1, 0) + jnp.where(has_right, 1, 0)
    pl.semaphore_wait(barrier, peers - 1 + neighbours)
    loads[2].wait()

    @pl.when(has_right)
    def _():
        send_c.start()

    def odd_inverse(n):
        acc = product(lb, rb, n)
        x_own[n] = acc
        put_right_all(ra, n, acc)

    each(odd_inverse)

    @pl.when(has_right)
    def _():
        send_x.start()

    loads[1].wait()
    for n in range(chunks):
        for c in range(chunks):
            put_left(la, slice(c * LANES, (c + 1) * LANES), n, pair_block(c_even, c, n))
            put_right(rb, c, n, adjoint_block(c_even, c, n))

    each(lambda n: put_left(lb, every, n, product(la, ra, n)))

    @pl.when(has_left)
    def _():
        send_c.wait_recv()
        for n in range(chunks):
            for c in range(chunks):
                put_left(la, slice(c * LANES, (c + 1) * LANES), n, adjoint_block(c_odd_left, c, n))
                put_right(rc, c, n, pair_block(c_odd_left, c, n))
        send_x.wait_recv()

        def embed(n):
            put_right_all(ra, n, x_left[n])

        each(embed)

        def left_odd(n):
            acc = product(la, ra, n)
            lo_send[n] = acc
            put_left(lc, every, n, acc)

        each(left_odd)
        send_lo.start()

    loads[3].wait()
    for n in range(chunks):
        for c in range(chunks):
            reduced[n, c * LANES:(c + 1) * LANES, :] = pair_block(diag_even, c, n)

    def subtract_own(n):
        reduced[n] = reduced[n] - product(lb, rb, n)

    each(subtract_own)

    @pl.when(has_left)
    def _():
        def subtract_edge(n):
            reduced[n] = reduced[n] - product(lc, rc, n)

        each(subtract_edge)

    @pl.when(has_right)
    def _():
        for n in range(chunks):
            for c in range(chunks):
                put_right(rc, c, n, pair_block(c_odd, c, n))

        def upper(n):
            up_own[n] = product(lb, rc, n)

        each(upper)
        send_up.start()
        send_lo.wait_recv()

        def embed(n):
            put_left(lc, every, n, lo_recv[n])

        each(embed)

        def lower(n):
            low_own[n] = product(lc, rb, n)

        each(lower)
        send_low.start()

    prepare_inverse(lambda c, n: reduced[n, c * LANES:(c + 1) * LANES, :])
    each(residual)
    each(lambda n: put_right_all(ra, n, product(lb, rb, n)))

    @pl.when(has_right)
    def _():
        def embed(n):
            put_left(la, every, n, low_own[n])
            put_right_all(rb, n, up_own[n])

        each(embed)
        each(lambda n: put_left(lb, every, n, product(la, ra, n)))

        def lower_term(n):
            lt_send[n] = product(lb, rb, n)

        each(lower_term)
        send_lt.start()

    @pl.when(has_left)
    def _():
        send_up.wait_recv()
        send_low.wait_recv()

        def embed(n):
            put_left(la, every, n, up_left[n])
            put_right_all(rb, n, low_left[n])

        each(embed)
        each(lambda n: put_left(lb, every, n, product(la, ra, n)))

        def upper_term(n):
            ut_send[n] = product(lb, rb, n)

        each(upper_term)
        send_ut.start()

    @pl.when(has_left)
    def _():
        send_lt.wait_recv()

        def take(n):
            reduced[n] = reduced[n] - lt_recv[n]

        each(take)

    @pl.when(has_right)
    def _():
        send_ut.wait_recv()

        def take(n):
            reduced[n] = reduced[n] - ut_recv[n]

        each(take)

    prepare_inverse(lambda c, n: reduced[n, c * LANES:(c + 1) * LANES, :])

    def forward(n, peer, at):
        return pltpu.make_async_remote_copy(
            src_ref=gbuf.at[n, pl.ds(peer * rows, rows), :],
            dst_ref=rbuf.at[n, at],
            send_sem=f_send.at[n, peer],
            recv_sem=f_recv.at[n, at],
            device_id={"momentum": peer // energies, "energy": lax.rem(peer, energies)},
            device_id_type=MESH,
        )

    def backward(n, peer, at):
        return pltpu.make_async_remote_copy(
            src_ref=tbuf.at[n, peer],
            dst_ref=obuf.at[n, pl.ds(at * rows, rows), :],
            send_sem=b_send.at[n, peer],
            recv_sem=b_recv.at[n, at],
            device_id={"momentum": peer // energies, "energy": lax.rem(peer, energies)},
            device_id_type=MESH,
        )

    def around(fn):
        def step(d, carry):
            fn(lax.rem(here + d, peers))
            return carry

        lax.fori_loop(1, peers, step, 0)

    def finish(n):
        residual(n)
        gbuf[n] = product(lb, rb, n)
        around(lambda peer: forward(n, peer, here).start())
        rbuf[n, here] = gbuf[n, pl.ds(pl.multiple_of(here * rows, 8), rows), :]

    each(finish)

    transfers = transfer.shape[0]
    for q in range(transfers):
        mode = transfer[q]
        gain = strength[mode]
        moved = offset[mode]
        for e in range(energies):
            for f in range(energies):
                total = F32(0.0)
                for s in range(energies):
                    hits = jnp.where(s == e - moved, F32(1.0), F32(0.0)) + jnp.where(
                        s == e + moved, F32(1.0), F32(0.0)
                    )
                    total = total + hits * phonon[s, f]
                kern[(q * energies + e) * energies + f] = gain * total

    def combine(n):
        around(lambda peer: forward(n, here, peer).wait_recv())
        for k in range(momenta):
            for e in range(energies):
                total = None
                for source in range(momenta):
                    q = (k - source) % transfers
                    for f in range(energies):
                        term = kern[(q * energies + e) * energies + f] * rbuf[n, source * energies + f]
                        total = term if total is None else total + term
                tbuf[n, k * energies + e] = total
        around(lambda peer: backward(n, peer, here).start())
        obuf[n, pl.ds(pl.multiple_of(here * rows, 8), rows), :] = tbuf[n, here]

    each(combine)

    for n in range(chunks):
        around(lambda peer: backward(n, here, peer).wait_recv())
        columns = slice(n * LANES, (n + 1) * LANES)
        out[0, :, columns] = obuf[n, :, :LANES]
        out[1, :, columns] = obuf[n, :, LANES:]

    def drain(n):
        around(lambda peer: forward(n, peer, here).wait_send())
        around(lambda peer: backward(n, peer, here).wait_send())

    each(drain)

    @pl.when(has_right)
    def _():
        for copy in (send_c, send_x, send_up, send_low, send_lt):
            copy.wait_send()

    @pl.when(has_left)
    def _():
        for copy in (send_lo, send_ut):
            copy.wait_send()


def body(diag_blocks, couplings, phonon_matrix, mode_strength, transfer_mode, energy_offset):
    order = diag_blocks.shape[-1]
    chunks = order // LANES
    nodes = lax.axis_size("layer")
    energies = lax.axis_size("energy")
    momenta = lax.axis_size("momentum")
    peers = energies * momenta
    diag = diag_blocks.reshape(2, 2, order, order)
    coup = couplings.reshape(2, 2, order, order)
    plain = pltpu.VMEM((2, order, order), F32)
    chunked = pltpu.VMEM((chunks, order, 2 * LANES), F32)
    pieces = pltpu.VMEM((chunks, peers, order // peers, 2 * LANES), F32)
    left = pltpu.VMEM((order, 2 * order), BF16)
    right = pltpu.VMEM((chunks, 2 * order, 2 * LANES), BF16)
    smem = pl.BlockSpec(memory_space=pltpu.SMEM)
    anywhere = pl.BlockSpec(memory_space=pl.ANY)
    transfers = transfer_mode.shape[0]
    dma = pltpu.SemaphoreType.DMA
    result = pl.pallas_call(
        partial(kernel, chunks, nodes, energies, momenta),
        out_shape=jax.ShapeDtypeStruct((2, order, order), F32),
        in_specs=[anywhere, anywhere, smem, smem, smem, smem],
        out_specs=pl.BlockSpec(memory_space=pltpu.VMEM),
        scratch_shapes=[plain] * 5 + [chunked] * 13 + [chunked, pieces, pieces, chunked]
        + [pltpu.SMEM((transfers * energies * energies,), F32)]
        + [left] * 6 + [right] * 6
        + [dma((4,)), dma((7,)), dma((7,))] + [dma((chunks, peers))] * 4,
        compiler_params=pltpu.CompilerParams(
            collective_id=0, has_side_effects=True, vmem_limit_bytes=60 * 1024 * 1024
        ),
    )(diag, coup, phonon_matrix, mode_strength, transfer_mode, energy_offset)
    return result[None, None, None]


def solution(mesh):
    return jax.shard_map(
        body,
        mesh=mesh,
        in_specs=(
            P("momentum", "layer", "energy", None, None, None),
            P("momentum", "layer", None, None, None),
            P(),
            P(),
            P(),
            P(),
        ),
        out_specs=P("momentum", "layer", "energy", None, None, None),
        check_vma=False,
    )
```

```python
from functools import partial

import jax
import jax.numpy as jnp
from jax import lax
from jax.experimental import pallas as pl
from jax.experimental.pallas import tpu as pltpu
from jax.sharding import PartitionSpec as P

MESH = pl.DeviceIdType.MESH
F32 = jnp.float32
BF16 = jnp.bfloat16
LANES = 128


def split(value):
    high = value.astype(BF16)
    low = (value - high.astype(F32)).astype(BF16)
    return high, low


def put_left(left, rows, n, value):
    columns = pl.ds(n * 2 * LANES, 2 * LANES)
    for ref, part in zip(left, split(value)):
        ref[rows, columns] = part


def put_right(right, c, n, value):
    for ref, part in zip(right, split(value)):
        base = c * 2 * LANES
        ref[n, base:base + LANES, :] = part
        ref[n, base + LANES:base + 2 * LANES, :LANES] = -part[:, LANES:]
        ref[n, base + LANES:base + 2 * LANES, LANES:] = part[:, :LANES]


def put_right_all(right, n, value):
    for c in range(value.shape[0] // LANES):
        put_right(right, c, n, value[c * LANES:(c + 1) * LANES])


def dot(a, b):
    return jnp.dot(a, b, preferred_element_type=F32)


def product(left, right, n):
    right_high, right_low = right[0][n], right[1][n]
    parts = []
    for m in range(0, left[0].shape[0], LANES):
        left_high, left_low = left[0][m:m + LANES, :], left[1][m:m + LANES, :]
        parts.append(
            dot(left_high, right_high) + dot(left_high, right_low) + dot(left_low, right_high)
        )
    return jnp.concatenate(parts, axis=0)


def kernel(
    chunks, nodes, energies, momenta,
    diag, coup, phonon, strength, transfer, offset, out,
    diag_odd, diag_even, c_even, c_odd, c_odd_left,
    x_own, x_left, lo_send, lo_recv, up_own, up_left, low_own, low_left,
    lt_send, lt_recv, ut_send, ut_recv, reduced, gbuf, rbuf, tbuf, obuf, kern,
    la_h, la_l, lb_h, lb_l, lc_h, lc_l,
    ra_h, ra_l, rb_h, rb_l, rc_h, rc_l,
    in_sem, l_send, l_recv, f_send, f_recv, b_send, b_recv,
):
    la, lb, lc = (la_h, la_l), (lb_h, lb_l), (lc_h, lc_l)
    ra, rb, rc = (ra_h, ra_l), (rb_h, rb_l), (rc_h, rc_l)
    order = chunks * LANES
    me = lax.axis_index("layer")
    here_k = lax.axis_index("momentum")
    here_e = lax.axis_index("energy")
    peers = energies * momenta
    here = here_k * energies + here_e
    rows = order // peers
    has_right = me < nodes - 1
    has_left = me > 0

    loads = []
    for s, (src, dst) in enumerate(
        ((diag.at[1], diag_odd), (coup.at[0], c_even), (coup.at[1], c_odd), (diag.at[0], diag_even))
    ):
        load = pltpu.make_async_copy(src, dst, in_sem.at[s])
        load.start()
        loads.append(load)

    barrier = pltpu.get_barrier_semaphore()

    @pl.when(has_right)
    def _():
        pl.semaphore_signal(barrier, inc=1, device_id={"layer": me + 1}, device_id_type=MESH)

    @pl.when(has_left)
    def _():
        pl.semaphore_signal(barrier, inc=1, device_id={"layer": me - 1}, device_id_type=MESH)

    def greet(d, carry):
        peer = lax.rem(here + d, peers)
        pl.semaphore_signal(
            barrier, inc=1,
            device_id={"momentum": peer // energies, "energy": lax.rem(peer, energies)},
            device_id_type=MESH,
        )
        return carry

    lax.fori_loop(1, peers, greet, 0)

    def to_layer(slot, src, dst, step):
        return lambda n: pltpu.make_async_remote_copy(
            src_ref=src.at[n], dst_ref=dst.at[n],
            send_sem=l_send.at[slot, n], recv_sem=l_recv.at[slot, n],
            device_id={"layer": me + step}, device_id_type=MESH,
        )

    send_c = to_layer(0, c_odd, c_odd_left, 1)
    send_x = to_layer(1, x_own, x_left, 1)
    send_lo = to_layer(2, lo_send, lo_recv, -1)
    send_up = to_layer(3, up_own, up_left, 1)
    send_low = to_layer(4, low_own, low_left, 1)
    send_lt = to_layer(5, lt_send, lt_recv, 1)
    send_ut = to_layer(6, ut_send, ut_recv, -1)

    eye = (
        lax.broadcasted_iota(jnp.int32, (LANES, LANES), 0)
        == lax.broadcasted_iota(jnp.int32, (LANES, LANES), 1)
    )
    two = jnp.where(eye, F32(2.0), F32(0.0))

    def prepare_inverse(read):
        row_inv, col_inv = [], []
        for c in range(chunks):
            block = read(c, c)
            real = jnp.where(eye, block[:, :LANES], 0.0)
            imag = jnp.where(eye, block[:, LANES:], 0.0)
            for axis, found in ((0, row_inv), (1, col_inv)):
                r = jnp.sum(real, axis=axis, keepdims=True)
                i = jnp.sum(imag, axis=axis, keepdims=True)
                modulus = r * r + i * i
                found.append((r / modulus, -i / modulus))
        for n in range(chunks):
            for c in range(chunks):
                block = read(c, n)
                put_left(la, slice(c * LANES, (c + 1) * LANES), n, block)
                a_r, a_i = block[:, :LANES], block[:, LANES:]
                x_r, x_i = row_inv[n]
                y_r, y_i = col_inv[c]
                res_r = a_i * x_i - a_r * x_r
                if c == n:
                    res_r = res_r + two
                res_i = -(a_r * x_i + a_i * x_r)
                first = jnp.concatenate(
                    [y_r * res_r - y_i * res_i, y_r * res_i + y_i * res_r], axis=1
                )
                put_left(lb, slice(c * LANES, (c + 1) * LANES), n, first)
                put_right(ra, c, n, first)

    def residual(n):
        acc = product(la, ra, n)
        for c in range(chunks):
            block = -acc[c * LANES:(c + 1) * LANES]
            if c == n:
                block = jnp.concatenate([two + block[:, :LANES], block[:, LANES:]], axis=1)
            put_right(rb, c, n, block)

    def each(fn):
        for n in range(chunks):
            fn(n)

    def loop(fn):
        lax.fori_loop(0, chunks, lambda n, carry: (fn(n), carry)[1], 0)

    def pair_block(ref, c, n):
        rs, cs = slice(c * LANES, (c + 1) * LANES), slice(n * LANES, (n + 1) * LANES)
        return jnp.concatenate([ref[0, rs, cs], ref[1, rs, cs]], axis=1)

    def adjoint_block(ref, c, n):
        rs, cs = slice(n * LANES, (n + 1) * LANES), slice(c * LANES, (c + 1) * LANES)
        return jnp.concatenate([ref[0, rs, cs].T, -ref[1, rs, cs].T], axis=1)

    every = slice(0, order)

    loads[0].wait()
    prepare_inverse(lambda c, n: pair_block(diag_odd, c, n))
    each(residual)

    neighbours = jnp.where(has_left, 1, 0) + jnp.where(has_right, 1, 0)
    pl.semaphore_wait(barrier, peers - 1 + neighbours)
    loads[2].wait()

    @pl.when(has_right)
    def _():
        send_c(0).start()
        send_c(1).start()

    def odd_inverse(n):
        acc = product(lb, rb, n)
        x_own[n] = acc

        @pl.when(has_right)
        def _():
            send_x(n).start()

        put_right_all(ra, n, acc)

    each(odd_inverse)

    loads[1].wait()
    for n in range(chunks):
        for c in range(chunks):
            put_left(la, slice(c * LANES, (c + 1) * LANES), n, pair_block(c_even, c, n))
            put_right(rb, c, n, adjoint_block(c_even, c, n))

    each(lambda n: put_left(lb, every, n, product(la, ra, n)))

    @pl.when(has_left)
    def _():
        send_c(0).wait_recv()
        send_c(1).wait_recv()
        for n in range(chunks):
            for c in range(chunks):
                put_left(la, slice(c * LANES, (c + 1) * LANES), n, adjoint_block(c_odd_left, c, n))
                put_right(rc, c, n, pair_block(c_odd_left, c, n))

        def embed(n):
            send_x(n).wait_recv()
            put_right_all(ra, n, x_left[n])

        each(embed)

        def left_odd(n):
            acc = product(la, ra, n)
            lo_send[n] = acc
            send_lo(n).start()
            put_left(lc, every, n, acc)

        each(left_odd)

    loads[3].wait()
    for n in range(chunks):
        for c in range(chunks):
            reduced[n, c * LANES:(c + 1) * LANES, :] = pair_block(diag_even, c, n)

    def subtract_own(n):
        reduced[n] = reduced[n] - product(lb, rb, n)

    each(subtract_own)

    @pl.when(has_left)
    def _():
        def subtract_edge(n):
            reduced[n] = reduced[n] - product(lc, rc, n)

        each(subtract_edge)

    @pl.when(has_right)
    def _():
        for n in range(chunks):
            for c in range(chunks):
                put_right(rc, c, n, pair_block(c_odd, c, n))

        def upper(n):
            up_own[n] = product(lb, rc, n)
            send_up(n).start()

        each(upper)

        def embed(n):
            send_lo(n).wait_recv()
            put_left(lc, every, n, lo_recv[n])

        each(embed)

        def lower(n):
            low_own[n] = product(lc, rb, n)
            send_low(n).start()

        each(lower)

    prepare_inverse(lambda c, n: reduced[n, c * LANES:(c + 1) * LANES, :])
    each(residual)
    each(lambda n: put_right_all(ra, n, product(lb, rb, n)))

    @pl.when(has_right)
    def _():
        def embed(n):
            put_left(la, every, n, low_own[n])
            put_right_all(rb, n, up_own[n])

        each(embed)
        each(lambda n: put_left(lb, every, n, product(la, ra, n)))

        def lower_term(n):
            lt_send[n] = product(lb, rb, n)
            send_lt(n).start()

        each(lower_term)

    @pl.when(has_left)
    def _():

        def embed(n):
            send_up(n).wait_recv()
            send_low(n).wait_recv()
            put_left(la, every, n, up_left[n])
            put_right_all(rb, n, low_left[n])

        each(embed)
        each(lambda n: put_left(lb, every, n, product(la, ra, n)))

        def upper_term(n):
            ut_send[n] = product(lb, rb, n)
            send_ut(n).start()

        each(upper_term)

    @pl.when(has_left)
    def _():

        def take(n):
            send_lt(n).wait_recv()
            reduced[n] = reduced[n] - lt_recv[n]

        each(take)

    @pl.when(has_right)
    def _():

        def take(n):
            send_ut(n).wait_recv()
            reduced[n] = reduced[n] - ut_recv[n]

        each(take)

    prepare_inverse(lambda c, n: reduced[n, c * LANES:(c + 1) * LANES, :])

    def forward(n, peer, at):
        return pltpu.make_async_remote_copy(
            src_ref=gbuf.at[n, pl.ds(peer * rows, rows), :],
            dst_ref=rbuf.at[n, at],
            send_sem=f_send.at[n, peer],
            recv_sem=f_recv.at[n, at],
            device_id={"momentum": peer // energies, "energy": lax.rem(peer, energies)},
            device_id_type=MESH,
        )

    def backward(n, peer, at):
        return pltpu.make_async_remote_copy(
            src_ref=tbuf.at[n, peer],
            dst_ref=obuf.at[n, pl.ds(at * rows, rows), :],
            send_sem=b_send.at[n, peer],
            recv_sem=b_recv.at[n, at],
            device_id={"momentum": peer // energies, "energy": lax.rem(peer, energies)},
            device_id_type=MESH,
        )

    def around(fn):
        def step(d, carry):
            fn(lax.rem(here + d, peers))
            return carry

        lax.fori_loop(1, peers, step, 0)

    def finish(n):
        residual(n)
        gbuf[n] = product(lb, rb, n)
        around(lambda peer: forward(n, peer, here).start())
        rbuf[n, here] = gbuf[n, pl.ds(pl.multiple_of(here * rows, 8), rows), :]

    each(finish)

    transfers = transfer.shape[0]
    for q in range(transfers):
        mode = transfer[q]
        gain = strength[mode]
        moved = offset[mode]
        for e in range(energies):
            for f in range(energies):
                total = F32(0.0)
                for s in range(energies):
                    hits = jnp.where(s == e - moved, F32(1.0), F32(0.0)) + jnp.where(
                        s == e + moved, F32(1.0), F32(0.0)
                    )
                    total = total + hits * phonon[s, f]
                kern[(q * energies + e) * energies + f] = gain * total

    def combine(n):
        around(lambda peer: forward(n, here, peer).wait_recv())
        for k in range(momenta):
            for e in range(energies):
                total = None
                for source in range(momenta):
                    q = (k - source) % transfers
                    for f in range(energies):
                        term = kern[(q * energies + e) * energies + f] * rbuf[n, source * energies + f]
                        total = term if total is None else total + term
                tbuf[n, k * energies + e] = total
        around(lambda peer: backward(n, peer, here).start())
        obuf[n, pl.ds(pl.multiple_of(here * rows, 8), rows), :] = tbuf[n, here]

    loop(combine)

    for n in range(chunks):
        around(lambda peer: backward(n, here, peer).wait_recv())
        columns = slice(n * LANES, (n + 1) * LANES)
        out[0, :, columns] = obuf[n, :, :LANES]
        out[1, :, columns] = obuf[n, :, LANES:]

    def drain(n):
        around(lambda peer: forward(n, peer, here).wait_send())
        around(lambda peer: backward(n, peer, here).wait_send())

    loop(drain)

    @pl.when(has_right)
    def _():
        for n in range(2):
            send_c(n).wait_send()
        for send in (send_x, send_up, send_low, send_lt):
            each(lambda n: send(n).wait_send())

    @pl.when(has_left)
    def _():
        for send in (send_lo, send_ut):
            each(lambda n: send(n).wait_send())


def body(diag_blocks, couplings, phonon_matrix, mode_strength, transfer_mode, energy_offset):
    order = diag_blocks.shape[-1]
    chunks = order // LANES
    nodes = lax.axis_size("layer")
    energies = lax.axis_size("energy")
    momenta = lax.axis_size("momentum")
    peers = energies * momenta
    diag = diag_blocks.reshape(2, 2, order, order)
    coup = couplings.reshape(2, 2, order, order)
    plain = pltpu.VMEM((2, order, order), F32)
    chunked = pltpu.VMEM((chunks, order, 2 * LANES), F32)
    pieces = pltpu.VMEM((chunks, peers, order // peers, 2 * LANES), F32)
    left = pltpu.VMEM((order, 2 * order), BF16)
    right = pltpu.VMEM((chunks, 2 * order, 2 * LANES), BF16)
    smem = pl.BlockSpec(memory_space=pltpu.SMEM)
    anywhere = pl.BlockSpec(memory_space=pl.ANY)
    transfers = transfer_mode.shape[0]
    dma = pltpu.SemaphoreType.DMA
    result = pl.pallas_call(
        partial(kernel, chunks, nodes, energies, momenta),
        out_shape=jax.ShapeDtypeStruct((2, order, order), F32),
        in_specs=[anywhere, anywhere, smem, smem, smem, smem],
        out_specs=pl.BlockSpec(memory_space=pltpu.VMEM),
        scratch_shapes=[plain] * 5 + [chunked] * 13 + [chunked, pieces, pieces, chunked]
        + [pltpu.SMEM((transfers * energies * energies,), F32)]
        + [left] * 6 + [right] * 6
        + [dma((4,))] + [dma((7, max(2, chunks)))] * 2 + [dma((chunks, peers))] * 4,
        compiler_params=pltpu.CompilerParams(
            collective_id=0, has_side_effects=True, vmem_limit_bytes=60 * 1024 * 1024
        ),
    )(diag, coup, phonon_matrix, mode_strength, transfer_mode, energy_offset)
    return result[None, None, None]


def solution(mesh):
    return jax.shard_map(
        body,
        mesh=mesh,
        in_specs=(
            P("momentum", "layer", "energy", None, None, None),
            P("momentum", "layer", None, None, None),
            P(),
            P(),
            P(),
            P(),
        ),
        out_specs=P("momentum", "layer", "energy", None, None, None),
        check_vma=False,
    )
```

```python
from functools import partial

import jax
import jax.numpy as jnp
from jax import lax
from jax.experimental import pallas as pl
from jax.experimental.pallas import tpu as pltpu
from jax.sharding import PartitionSpec as P

MESH = pl.DeviceIdType.MESH
F32 = jnp.float32
BF16 = jnp.bfloat16
LANES = 128


def split(value):
    high = value.astype(BF16)
    low = (value - high.astype(F32)).astype(BF16)
    return high, low


def put_left(left, rows, n, value):
    columns = pl.ds(n * 2 * LANES, 2 * LANES)
    for ref, part in zip(left, split(value)):
        ref[rows, columns] = part


def put_right(right, c, n, value):
    for ref, part in zip(right, split(value)):
        base = c * 2 * LANES
        ref[n, base:base + LANES, :] = part
        ref[n, base + LANES:base + 2 * LANES, :LANES] = -part[:, LANES:]
        ref[n, base + LANES:base + 2 * LANES, LANES:] = part[:, :LANES]


def put_right_all(right, n, value):
    for c in range(value.shape[0] // LANES):
        put_right(right, c, n, value[c * LANES:(c + 1) * LANES])


def dot(a, b):
    return jnp.dot(a, b, preferred_element_type=F32)


def product(left, right, n):
    right_high, right_low = right[0][n], right[1][n]
    parts = []
    for m in range(0, left[0].shape[0], LANES):
        left_high, left_low = left[0][m:m + LANES, :], left[1][m:m + LANES, :]
        parts.append(
            dot(left_high, right_high) + dot(left_high, right_low) + dot(left_low, right_high)
        )
    return jnp.concatenate(parts, axis=0)


def kernel(
    chunks, nodes, energies, momenta,
    diag, coup, phonon, strength, transfer, offset, out,
    diag_odd, diag_even, c_even, c_odd, c_odd_left,
    x_own, x_left, lo_send, lo_recv, up_own, up_left, low_own, low_left,
    lt_send, lt_recv, ut_send, ut_recv, reduced, gbuf, rbuf, tbuf, obuf, kern,
    la_h, la_l, lb_h, lb_l, lc_h, lc_l,
    ra_h, ra_l, rb_h, rb_l, rc_h, rc_l,
    in_sem, l_send, l_recv, f_send, f_recv, b_send, b_recv,
):
    la, lb, lc = (la_h, la_l), (lb_h, lb_l), (lc_h, lc_l)
    ra, rb, rc = (ra_h, ra_l), (rb_h, rb_l), (rc_h, rc_l)
    order = chunks * LANES
    me = lax.axis_index("layer")
    here_k = lax.axis_index("momentum")
    here_e = lax.axis_index("energy")
    peers = energies * momenta
    here = here_k * energies + here_e
    rows = order // peers
    has_right = me < nodes - 1
    has_left = me > 0

    loads = []
    for s, (src, dst) in enumerate(
        ((diag.at[1], diag_odd), (coup.at[0], c_even), (coup.at[1], c_odd), (diag.at[0], diag_even))
    ):
        load = pltpu.make_async_copy(src, dst, in_sem.at[s])
        load.start()
        loads.append(load)

    barrier = pltpu.get_barrier_semaphore()

    @pl.when(has_right)
    def _():
        pl.semaphore_signal(barrier, inc=1, device_id={"layer": me + 1}, device_id_type=MESH)

    @pl.when(has_left)
    def _():
        pl.semaphore_signal(barrier, inc=1, device_id={"layer": me - 1}, device_id_type=MESH)

    def greet(d, carry):
        peer = lax.rem(here + d, peers)
        pl.semaphore_signal(
            barrier, inc=1,
            device_id={"momentum": peer // energies, "energy": lax.rem(peer, energies)},
            device_id_type=MESH,
        )
        return carry

    lax.fori_loop(1, peers, greet, 0)

    def to_layer(slot, src, dst, step):
        return lambda n: pltpu.make_async_remote_copy(
            src_ref=src.at[n], dst_ref=dst.at[n],
            send_sem=l_send.at[slot, n], recv_sem=l_recv.at[slot, n],
            device_id={"layer": me + step}, device_id_type=MESH,
        )

    send_c = to_layer(0, c_odd, c_odd_left, 1)
    send_x = to_layer(1, x_own, x_left, 1)
    send_lo = to_layer(2, lo_send, lo_recv, -1)
    send_up = to_layer(3, up_own, up_left, 1)
    send_low = to_layer(4, low_own, low_left, 1)
    send_lt = to_layer(5, lt_send, lt_recv, 1)
    send_ut = to_layer(6, ut_send, ut_recv, -1)

    eye = (
        lax.broadcasted_iota(jnp.int32, (LANES, LANES), 0)
        == lax.broadcasted_iota(jnp.int32, (LANES, LANES), 1)
    )
    two = jnp.where(eye, F32(2.0), F32(0.0))

    def prepare_inverse(read):
        row_inv, col_inv = [], []
        for c in range(chunks):
            block = read(c, c)
            real = jnp.where(eye, block[:, :LANES], 0.0)
            imag = jnp.where(eye, block[:, LANES:], 0.0)
            for axis, found in ((0, row_inv), (1, col_inv)):
                r = jnp.sum(real, axis=axis, keepdims=True)
                i = jnp.sum(imag, axis=axis, keepdims=True)
                modulus = r * r + i * i
                found.append((r / modulus, -i / modulus))
        for n in range(chunks):
            for c in range(chunks):
                block = read(c, n)
                put_left(la, slice(c * LANES, (c + 1) * LANES), n, block)
                a_r, a_i = block[:, :LANES], block[:, LANES:]
                x_r, x_i = row_inv[n]
                y_r, y_i = col_inv[c]
                res_r = a_i * x_i - a_r * x_r
                if c == n:
                    res_r = res_r + two
                res_i = -(a_r * x_i + a_i * x_r)
                first = jnp.concatenate(
                    [y_r * res_r - y_i * res_i, y_r * res_i + y_i * res_r], axis=1
                )
                put_left(lb, slice(c * LANES, (c + 1) * LANES), n, first)
                put_right(ra, c, n, first)

    def residual(n):
        acc = product(la, ra, n)
        for c in range(chunks):
            block = -acc[c * LANES:(c + 1) * LANES]
            if c == n:
                block = jnp.concatenate([two + block[:, :LANES], block[:, LANES:]], axis=1)
            put_right(rb, c, n, block)

    def each(fn):
        for n in range(chunks):
            fn(n)

    def loop(fn):
        lax.fori_loop(0, chunks, lambda n, carry: (fn(n), carry)[1], 0)

    def pair_block(ref, c, n):
        rs, cs = slice(c * LANES, (c + 1) * LANES), slice(n * LANES, (n + 1) * LANES)
        return jnp.concatenate([ref[0, rs, cs], ref[1, rs, cs]], axis=1)

    def adjoint_block(ref, c, n):
        rs, cs = slice(n * LANES, (n + 1) * LANES), slice(c * LANES, (c + 1) * LANES)
        return jnp.concatenate([ref[0, rs, cs].T, -ref[1, rs, cs].T], axis=1)

    every = slice(0, order)

    loads[0].wait()
    prepare_inverse(lambda c, n: pair_block(diag_odd, c, n))
    each(residual)

    def odd_inverse(n):
        acc = product(lb, rb, n)
        x_own[n] = acc
        put_right_all(ra, n, acc)

    each(odd_inverse)

    loads[1].wait()
    for n in range(chunks):
        for c in range(chunks):
            put_left(la, slice(c * LANES, (c + 1) * LANES), n, pair_block(c_even, c, n))
            put_right(rb, c, n, adjoint_block(c_even, c, n))

    each(lambda n: put_left(lb, every, n, product(la, ra, n)))

    neighbours = jnp.where(has_left, 1, 0) + jnp.where(has_right, 1, 0)
    pl.semaphore_wait(barrier, peers - 1 + neighbours)
    loads[2].wait()

    @pl.when(has_right)
    def _():
        send_c(0).start()
        send_c(1).start()
        each(lambda n: send_x(n).start())

    loads[3].wait()
    for n in range(chunks):
        for c in range(chunks):
            reduced[n, c * LANES:(c + 1) * LANES, :] = pair_block(diag_even, c, n)

    def subtract_own(n):
        reduced[n] = reduced[n] - product(lb, rb, n)

    each(subtract_own)

    @pl.when(has_left)
    def _():
        send_c(0).wait_recv()
        send_c(1).wait_recv()
        for n in range(chunks):
            for c in range(chunks):
                put_left(la, slice(c * LANES, (c + 1) * LANES), n, adjoint_block(c_odd_left, c, n))
                put_right(rc, c, n, pair_block(c_odd_left, c, n))

        def embed(n):
            send_x(n).wait_recv()
            put_right_all(ra, n, x_left[n])

        each(embed)

        def left_odd(n):
            acc = product(la, ra, n)
            lo_send[n] = acc
            send_lo(n).start()
            put_left(lc, every, n, acc)

        each(left_odd)

    @pl.when(has_left)
    def _():
        def subtract_edge(n):
            reduced[n] = reduced[n] - product(lc, rc, n)

        each(subtract_edge)

    @pl.when(has_right)
    def _():
        for n in range(chunks):
            for c in range(chunks):
                put_right(rc, c, n, pair_block(c_odd, c, n))

        def upper(n):
            up_own[n] = product(lb, rc, n)
            send_up(n).start()

        each(upper)

        def embed(n):
            send_lo(n).wait_recv()
            put_left(lc, every, n, lo_recv[n])

        each(embed)

        def lower(n):
            low_own[n] = product(lc, rb, n)
            send_low(n).start()

        each(lower)

    prepare_inverse(lambda c, n: reduced[n, c * LANES:(c + 1) * LANES, :])
    each(residual)
    each(lambda n: put_right_all(ra, n, product(lb, rb, n)))

    @pl.when(has_right)
    def _():
        def embed(n):
            put_left(la, every, n, low_own[n])
            put_right_all(rb, n, up_own[n])

        each(embed)
        each(lambda n: put_left(lb, every, n, product(la, ra, n)))

        def lower_term(n):
            lt_send[n] = product(lb, rb, n)
            send_lt(n).start()

        each(lower_term)

    @pl.when(has_left)
    def _():

        def embed(n):
            send_up(n).wait_recv()
            send_low(n).wait_recv()
            put_left(la, every, n, up_left[n])
            put_right_all(rb, n, low_left[n])

        each(embed)
        each(lambda n: put_left(lb, every, n, product(la, ra, n)))

        def upper_term(n):
            ut_send[n] = product(lb, rb, n)
            send_ut(n).start()

        each(upper_term)

    @pl.when(has_left)
    def _():

        def take(n):
            send_lt(n).wait_recv()
            reduced[n] = reduced[n] - lt_recv[n]

        each(take)

    @pl.when(has_right)
    def _():

        def take(n):
            send_ut(n).wait_recv()
            reduced[n] = reduced[n] - ut_recv[n]

        each(take)

    prepare_inverse(lambda c, n: reduced[n, c * LANES:(c + 1) * LANES, :])

    def forward(n, peer, at):
        return pltpu.make_async_remote_copy(
            src_ref=gbuf.at[n, pl.ds(peer * rows, rows), :],
            dst_ref=rbuf.at[n, at],
            send_sem=f_send.at[n, peer],
            recv_sem=f_recv.at[n, at],
            device_id={"momentum": peer // energies, "energy": lax.rem(peer, energies)},
            device_id_type=MESH,
        )

    def backward(n, peer, at):
        return pltpu.make_async_remote_copy(
            src_ref=tbuf.at[n, peer],
            dst_ref=obuf.at[n, pl.ds(at * rows, rows), :],
            send_sem=b_send.at[n, peer],
            recv_sem=b_recv.at[n, at],
            device_id={"momentum": peer // energies, "energy": lax.rem(peer, energies)},
            device_id_type=MESH,
        )

    def around(fn):
        def step(d, carry):
            fn(lax.rem(here + d, peers))
            return carry

        lax.fori_loop(1, peers, step, 0)

    def finish(n):
        residual(n)
        gbuf[n] = product(lb, rb, n)
        around(lambda peer: forward(n, peer, here).start())
        rbuf[n, here] = gbuf[n, pl.ds(pl.multiple_of(here * rows, 8), rows), :]

    each(finish)

    transfers = transfer.shape[0]
    for q in range(transfers):
        mode = transfer[q]
        gain = strength[mode]
        moved = offset[mode]
        for e in range(energies):
            for f in range(energies):
                total = F32(0.0)
                for s in range(energies):
                    hits = jnp.where(s == e - moved, F32(1.0), F32(0.0)) + jnp.where(
                        s == e + moved, F32(1.0), F32(0.0)
                    )
                    total = total + hits * phonon[s, f]
                kern[(q * energies + e) * energies + f] = gain * total

    def combine(n):
        around(lambda peer: forward(n, here, peer).wait_recv())
        for k in range(momenta):
            for e in range(energies):
                total = None
                for source in range(momenta):
                    q = (k - source) % transfers
                    for f in range(energies):
                        term = kern[(q * energies + e) * energies + f] * rbuf[n, source * energies + f]
                        total = term if total is None else total + term
                tbuf[n, k * energies + e] = total
        around(lambda peer: backward(n, peer, here).start())
        obuf[n, pl.ds(pl.multiple_of(here * rows, 8), rows), :] = tbuf[n, here]

    loop(combine)

    for n in range(chunks):
        around(lambda peer: backward(n, here, peer).wait_recv())
        columns = slice(n * LANES, (n + 1) * LANES)
        out[0, :, columns] = obuf[n, :, :LANES]
        out[1, :, columns] = obuf[n, :, LANES:]

    def drain(n):
        around(lambda peer: forward(n, peer, here).wait_send())
        around(lambda peer: backward(n, peer, here).wait_send())

    loop(drain)

    @pl.when(has_right)
    def _():
        for n in range(2):
            send_c(n).wait_send()
        for send in (send_x, send_up, send_low, send_lt):
            each(lambda n: send(n).wait_send())

    @pl.when(has_left)
    def _():
        for send in (send_lo, send_ut):
            each(lambda n: send(n).wait_send())


def body(diag_blocks, couplings, phonon_matrix, mode_strength, transfer_mode, energy_offset):
    order = diag_blocks.shape[-1]
    chunks = order // LANES
    nodes = lax.axis_size("layer")
    energies = lax.axis_size("energy")
    momenta = lax.axis_size("momentum")
    peers = energies * momenta
    diag = diag_blocks.reshape(2, 2, order, order)
    coup = couplings.reshape(2, 2, order, order)
    plain = pltpu.VMEM((2, order, order), F32)
    chunked = pltpu.VMEM((chunks, order, 2 * LANES), F32)
    pieces = pltpu.VMEM((chunks, peers, order // peers, 2 * LANES), F32)
    left = pltpu.VMEM((order, 2 * order), BF16)
    right = pltpu.VMEM((chunks, 2 * order, 2 * LANES), BF16)
    smem = pl.BlockSpec(memory_space=pltpu.SMEM)
    anywhere = pl.BlockSpec(memory_space=pl.ANY)
    transfers = transfer_mode.shape[0]
    dma = pltpu.SemaphoreType.DMA
    result = pl.pallas_call(
        partial(kernel, chunks, nodes, energies, momenta),
        out_shape=jax.ShapeDtypeStruct((2, order, order), F32),
        in_specs=[anywhere, anywhere, smem, smem, smem, smem],
        out_specs=pl.BlockSpec(memory_space=pltpu.VMEM),
        scratch_shapes=[plain] * 5 + [chunked] * 13 + [chunked, pieces, pieces, chunked]
        + [pltpu.SMEM((transfers * energies * energies,), F32)]
        + [left] * 6 + [right] * 6
        + [dma((4,))] + [dma((7, max(2, chunks)))] * 2 + [dma((chunks, peers))] * 4,
        compiler_params=pltpu.CompilerParams(
            collective_id=0, has_side_effects=True, vmem_limit_bytes=60 * 1024 * 1024
        ),
    )(diag, coup, phonon_matrix, mode_strength, transfer_mode, energy_offset)
    return result[None, None, None]


def solution(mesh):
    return jax.shard_map(
        body,
        mesh=mesh,
        in_specs=(
            P("momentum", "layer", "energy", None, None, None),
            P("momentum", "layer", None, None, None),
            P(),
            P(),
            P(),
            P(),
        ),
        out_specs=P("momentum", "layer", "energy", None, None, None),
        check_vma=False,
    )
```
